32 devices in a mesh: dp: 16 (over z, y, core), tensor: 2 (over x).
Axes of the slice: x: 2, y: 2, z: 4, core: 2. Of those that a mesh axis runs over, the one named last changes fastest.
Arguments:
- images: float32 [48, 197, 768], P('dp'), may hold values from -60 to 60
- cotangent: float32 [48, 197, 768], P('dp'), may hold values from -6 to 6
- counts: int32 [16], replicated, may hold values from 1 to 3, 36 in all
- heads_weight: float32 [768, 3, 768], P('dp', None, 'tensor'), may hold values from -8 to 8
- heads_first: float32 [768, 3, 768], P('dp', None, 'tensor'), may hold values from -16 to 16
- heads_second: float32 [768, 3, 768], P('dp', None, 'tensor'), may hold values from 0.2 to 2
- merge_weight: float32 [768, 768], P('dp', 'tensor'), may hold values from -0.625 to 0.625
- merge_first: float32 [768, 768], P('dp', 'tensor'), may hold values from -16 to 16
- merge_second: float32 [768, 768], P('dp', 'tensor'), may hold values from 0.2 to 2
- expand_weight: float32 [768, 3072], P('dp', 'tensor'), may hold values from -0.21875 to 0.21875
- expand_first: float32 [768, 3072], P('dp', 'tensor'), may hold values from -16 to 16
- expand_second: float32 [768, 3072], P('dp', 'tensor'), may hold values from 0.2 to 2
- shrink_weight: float32 [768, 3072], P('dp', 'tensor'), may hold values from -0.109375 to 0.109375
- shrink_first: float32 [768, 3072], P('dp', 'tensor'), may hold values from -16 to 16
- shrink_second: float32 [768, 3072], P('dp', 'tensor'), may hold values from 0.2 to 2
- norm_gains: float32 [2, 768], replicated, may hold values from 0.5 to 1.5
- gains_first: float32 [2, 768], replicated, may hold values from -16 to 16
- gains_second: float32 [2, 768], replicated, may hold values from 0.2 to 2
- norm_shifts: float32 [2, 768], replicated, may hold values from -1.2 to 1.2
- shifts_first: float32 [2, 768], replicated, may hold values from -16 to 16
- shifts_second: float32 [2, 768], replicated, may hold values from 0.2 to 2
- branch_biases: float32 [2, 768], replicated, may hold values from -1.2 to 1.2
- branch_first: float32 [2, 768], replicated, may hold values from -16 to 16
- branch_second: float32 [2, 768], replicated, may hold values from 0.2 to 2
- attend_biases: float32 [2, 768], P(None, 'tensor'), may hold values from -1.2 to 1.2
- attend_first: float32 [2, 768], P(None, 'tensor'), may hold values from -16 to 16
- attend_second: float32 [2, 768], P(None, 'tensor'), may hold values from 0.2 to 2
- hidden_biases: float32 [3072], P('tensor'), may hold values from -1.2 to 1.2
- hidden_first: float32 [3072], P('tensor'), may hold values from -16 to 16
- hidden_second: float32 [3072], P('tensor'), may hold values from 0.2 to 2
Outputs:
- block_out: float32 [48, 197, 768], P('dp')
- input_grad: float32 [48, 197, 768], P('dp')
- heads_grad: float32 [768, 3, 768], P('dp', None, 'tensor')
- merge_grad: float32 [768, 768], P('dp', 'tensor')
- expand_grad: float32 [768, 3072], P('dp', 'tensor')
- shrink_grad: float32 [768, 3072], P('dp', 'tensor')
- gains_grad: float32 [2, 768], replicated
- shifts_grad: float32 [2, 768], replicated
- branch_grad: float32 [2, 768], replicated
- attend_grad: float32 [2, 768], P(None, 'tensor')
- hidden_grad: float32 [3072], P('tensor')
- heads_next: float32 [768, 3, 768], P('dp', None, 'tensor')
- merge_next: float32 [768, 768], P('dp', 'tensor')
- expand_next: float32 [768, 3072], P('dp', 'tensor')
- shrink_next: float32 [768, 3072], P('dp', 'tensor')
- gains_next: float32 [2, 768], replicated
- shifts_next: float32 [2, 768], replicated
- branch_next: float32 [2, 768], replicated
- attend_next: float32 [2, 768], P(None, 'tensor')
- hidden_next: float32 [3072], P('tensor')
- heads_mean: float32 [768, 3, 768], P('dp', None, 'tensor')
- merge_mean: float32 [768, 768], P('dp', 'tensor')
- expand_mean: float32 [768, 3072], P('dp', 'tensor')
- shrink_mean: float32 [768, 3072], P('dp', 'tensor')
- gains_mean: float32 [2, 768], replicated
- shifts_mean: float32 [2, 768], replicated
- branch_mean: float32 [2, 768], replicated
- attend_mean: float32 [2, 768], P(None, 'tensor')
- hidden_mean: float32 [3072], P('tensor')
- heads_square: float32 [768, 3, 768], P('dp', None, 'tensor')
- merge_square: float32 [768, 768], P('dp', 'tensor')
- expand_square: float32 [768, 3072], P('dp', 'tensor')
- shrink_square: float32 [768, 3072], P('dp', 'tensor')
- gains_square: float32 [2, 768], replicated
- shifts_square: float32 [2, 768], replicated
- branch_square: float32 [2, 768], replicated
- attend_square: float32 [2, 768], P(None, 'tensor')
- hidden_square: float32 [3072], P('tensor')
The draws below stay inside these ranges and needn't reach their ends.
Inputs may be any that keep to these rules, and one draw needn't show every extreme that they name: counts[i] images sit in the first counts[i] slots of dp index i; they add up to 36, and some index holds 3.
All inputs are finite; a program needn't handle non-finite values.
Results may differ from the reference program's by a relative error of at most 0.012.
The reference program's roundings to bfloat16 on the way count: a program that leaves them out, or rounds other values in their place, can miss the bound.
Values may be sent and summed in bfloat16 or wider, within the bound.
No kernel may reach another device: no remote copies, remote signals or barrier semaphores. Data moves between devices by JAX's collectives and lax.ppermute only.
A program may use at most 128 MiB of HBM per device.

```python
import math
import jax
import jax.numpy as jnp
import numpy as np
from jax import lax

D = 768
HEADS = 12
FF = 3072
SEQ = 197
IMG_CAP = 3
IMAGES = 36
SLOTS = 48
N_DP = 16


def draw_images(key, part):
    key_base, key_rows, key_cols = jax.random.split(key, 3)
    shape = (SLOTS, SEQ, D)
    row_scale = jnp.exp(jax.random.uniform(key_rows, (SLOTS, SEQ, 1), jnp.float32, 0.0, math.log(10.0)))
    col_scale = jnp.exp(jax.random.uniform(key_cols, (1, 1, D), jnp.float32, 0.0, math.log(10.0)))
    base = jax.random.truncated_normal(key_base, -6.0, 6.0, shape, jnp.float32)
    return base * row_scale * col_scale * 0.1


def draw_heads_weight(key, part):
    key_main = jax.random.fold_in(key, 0)
    spread = D ** (-0.5)
    base = jax.random.truncated_normal(key_main, -4.0, 4.0, (D, 3, D), jnp.float32) * spread
    return base


def strengthened(drawn, own_key, source, target, blocks, factor):
    owner, partner = [(jnp.arange(drawn.shape[dim]) // (drawn.shape[dim] // blocks)).reshape([-1 if axis == dim else 1 for axis in range(drawn.ndim)]) for dim in (source, target)]
    chosen = jax.random.permutation(own_key, blocks)[partner]
    strong = (owner == chosen) | (owner == (partner + blocks // 2) % blocks)
    return jnp.where(strong, factor * drawn, drawn)


def levels(own_key, extent, cuts, least, top_value):
    factor_of = 1.0
    for dim, parts in cuts:
        draws = jax.random.uniform(jax.random.fold_in(jax.random.fold_in(own_key, 6), dim), (parts,), jnp.float32, least / len(cuts), top_value / len(cuts))
        factor_of = factor_of * jnp.repeat(jnp.exp(draws), extent[dim] // parts).reshape((-1,) + (1,) * (len(extent) - 1 - dim))
    return factor_of


def length_profile(number_of, total, bound, skew):
    weights = [(1 << 20) // math.isqrt(standing ** skew) + 1 for standing in range(2, number_of + 1)]
    rest, given = total - bound - (number_of - 1), [1] * (number_of - 1)
    while rest > 0:
        candidates = [i for i in range(number_of - 1) if given[i] < bound]
        mass, remaining = sum([weights[i] for i in candidates]), rest
        for i in candidates:
            addition = min(bound - given[i], max(1, remaining * weights[i] // mass), rest)
            given[i] = given[i] + addition
            rest = rest - addition
    return np.array([bound] + given)


def ragged(stream_key, count, total, reach, skew):
    if count == 2:
        one = jax.random.randint(stream_key, (), max(1, total - reach), min(reach, total - 1) + 1)
        return jnp.stack([one, total - one])
    lengths = jnp.asarray(length_profile(count, total, reach, skew), jnp.int32)
    twos = (count - 1) // 2
    giver, taker = lengths[1:1 + 2 * twos:2], lengths[2:2 + 2 * twos:2]
    slack = jnp.minimum(giver - 1, reach - taker)
    shifted = jax.random.randint(jax.random.fold_in(stream_key, 1), (twos,), 0, 1 << 20) % (slack + 1)
    lengths = lengths.at[1:1 + 2 * twos:2].set(giver - shifted).at[2:2 + 2 * twos:2].set(taker + shifted)
    return lengths[jax.random.permutation(jax.random.fold_in(stream_key, 2), count)]


def gaussian(stream_key, dims, width, limit, pieces=(), kind=jnp.bfloat16):
    values = width * jax.random.normal(stream_key, dims, jnp.float32)
    if pieces:
        values = values * levels(stream_key, dims, pieces, -0.22, 0.18)
    return jnp.clip(values, -limit, limit).astype(kind)


def gaussian_with(own_key, shape, scale, most, pieces, heavy, held_as=jnp.bfloat16):
    entries = scale * jax.random.normal(own_key, shape, jnp.float32)
    if pieces:
        entries = entries * levels(own_key, shape, pieces, -0.22, 0.18)
    return jnp.clip(strengthened(entries, jax.random.fold_in(own_key, 3), *heavy), -most, most).astype(held_as)


def setup_inputs(seed: int = 0) -> dict:
    arg_keys = jax.random.split(jax.random.key(seed), 31)
    return {
        "images": draw_images(jax.random.fold_in(arg_keys[30], 71), 0),
        "cotangent": gaussian_with(arg_keys[1], (SLOTS, SEQ, D), 1.0, 6.0, ((0, 16),), (0, 2, 16, 2.0), jnp.float32),
        "counts": ragged(arg_keys[2], N_DP, IMAGES, IMG_CAP, 2).astype(jnp.int32),
        "heads_weight": draw_heads_weight(jax.random.fold_in(arg_keys[30], 71), 0),
        "heads_first": gaussian(arg_keys[4], (D, 3, D), 3.0, 16.0, ((0, 16), (2, 2)), jnp.float32),
        "heads_second": jnp.clip(jnp.exp(math.log(2.0) - 2.3025851 * jax.random.uniform(arg_keys[5], (D, 3, D), jnp.float32) ** levels(arg_keys[5], (D, 3, D), ((0, 16), (2, 2)), -0.2, 0.2)), 0.2, 2.0),
        "merge_weight": gaussian(arg_keys[6], (D, D), (D // 8) ** -0.5, 0.625, ((0, 16), (1, 2)), jnp.float32),
        "merge_first": gaussian(arg_keys[7], (D, D), 3.0, 16.0, ((0, 16), (1, 2)), jnp.float32),
        "merge_second": jnp.clip(jnp.exp(math.log(2.0) - 2.3025851 * jax.random.uniform(arg_keys[8], (D, D), jnp.float32) ** levels(arg_keys[8], (D, D), ((0, 16), (1, 2)), -0.2, 0.2)), 0.2, 2.0),
        "expand_weight": gaussian(arg_keys[9], (D, FF), D ** -0.5, 0.21875, ((0, 16), (1, 2)), jnp.float32),
        "expand_first": gaussian(arg_keys[10], (D, FF), 3.0, 16.0, ((0, 16), (1, 2)), jnp.float32),
        "expand_second": jnp.clip(jnp.exp(math.log(2.0) - 2.3025851 * jax.random.uniform(arg_keys[11], (D, FF), jnp.float32) ** levels(arg_keys[11], (D, FF), ((0, 16), (1, 2)), -0.2, 0.2)), 0.2, 2.0),
        "shrink_weight": gaussian(arg_keys[12], (D, FF), FF ** -0.5, 0.109375, ((0, 16), (1, 2)), jnp.float32),
        "shrink_first": gaussian(arg_keys[13], (D, FF), 3.0, 16.0, ((0, 16), (1, 2)), jnp.float32),
        "shrink_second": jnp.clip(jnp.exp(math.log(2.0) - 2.3025851 * jax.random.uniform(arg_keys[14], (D, FF), jnp.float32) ** levels(arg_keys[14], (D, FF), ((0, 16), (1, 2)), -0.2, 0.2)), 0.2, 2.0),
        "norm_gains": jnp.clip(1.0 + 0.1 * jax.random.normal(arg_keys[15], (2, D), jnp.float32), 0.5, 1.5),
        "gains_first": gaussian(arg_keys[16], (2, D), 3.0, 16.0, (), jnp.float32),
        "gains_second": jnp.clip(jnp.exp(jax.random.uniform(arg_keys[17], (2, D), jnp.float32, math.log(0.2), math.log(2.0))), 0.2, 2.0),
        "norm_shifts": gaussian(arg_keys[18], (2, D), 0.2, 1.2, (), jnp.float32),
        "shifts_first": gaussian(arg_keys[19], (2, D), 3.0, 16.0, (), jnp.float32),
        "shifts_second": jnp.clip(jnp.exp(jax.random.uniform(arg_keys[20], (2, D), jnp.float32, math.log(0.2), math.log(2.0))), 0.2, 2.0),
        "branch_biases": gaussian(arg_keys[21], (2, D), 0.2, 1.2, (), jnp.float32),
        "branch_first": gaussian(arg_keys[22], (2, D), 3.0, 16.0, (), jnp.float32),
        "branch_second": jnp.clip(jnp.exp(jax.random.uniform(arg_keys[23], (2, D), jnp.float32, math.log(0.2), math.log(2.0))), 0.2, 2.0),
        "attend_biases": gaussian(arg_keys[24], (2, D), 0.2, 1.2, ((1, 2),), jnp.float32),
        "attend_first": gaussian(arg_keys[25], (2, D), 3.0, 16.0, ((1, 2),), jnp.float32),
        "attend_second": jnp.clip(jnp.exp(math.log(2.0) - 2.3025851 * jax.random.uniform(arg_keys[26], (2, D), jnp.float32) ** levels(arg_keys[26], (2, D), ((1, 2),), -0.2, 0.2)), 0.2, 2.0),
        "hidden_biases": gaussian(arg_keys[27], (FF,), 0.2, 1.2, ((0, 2),), jnp.float32),
        "hidden_first": gaussian(arg_keys[28], (FF,), 3.0, 16.0, ((0, 2),), jnp.float32),
        "hidden_second": jnp.clip(jnp.exp(math.log(2.0) - 2.3025851 * jax.random.uniform(arg_keys[29], (FF,), jnp.float32) ** levels(arg_keys[29], (FF,), ((0, 2),), -0.2, 0.2)), 0.2, 2.0),
    }


beta_one = 0.9
beta_two = 0.999
adam_epsilon = 1e-08
adam_steps = 2
matrix_rate = 0.02
vector_rate = 0.15
weight_decay = 0.1
norm_epsilon = 1e-06

def normalize(rows, gain, shift):
    centred = rows - lax.optimization_barrier(jnp.mean(rows, axis=-1, keepdims=True))
    inverse = lax.rsqrt(lax.optimization_barrier(jnp.mean(centred * centred, axis=-1, keepdims=True)) + norm_epsilon)
    unit = centred * inverse
    return (unit * gain + shift, unit, inverse)

def normalize_back(upstream, unit, inverse, gain):
    through = upstream * gain
    inner = through - lax.optimization_barrier(jnp.mean(through, axis=-1, keepdims=True)) - unit * lax.optimization_barrier(jnp.mean(through * unit, axis=-1, keepdims=True))
    return (inverse * inner, lax.optimization_barrier(jnp.sum(upstream * unit, axis=0)), lax.optimization_barrier(jnp.sum(upstream, axis=0)))

def gelu_exact(values):
    return jax.nn.gelu(values, approximate=False)

def adamw(weight, first, second, gradient, rate, decay_factor):
    first_new = beta_one * first + (1.0 - beta_one) * gradient
    second_new = beta_two * second + (1.0 - beta_two) * gradient * gradient
    first_hat = first_new / (1.0 - beta_one ** adam_steps)
    second_hat = second_new / (1.0 - beta_two ** adam_steps)
    weight_new = weight - rate * (first_hat / (jnp.sqrt(second_hat) + adam_epsilon) + decay_factor * weight)
    return (weight_new, first_new, second_new)

def image_pass(image, cotangent, live, matrices, norm_gains, norm_shifts, branch_biases, attend_biases, hidden_biases):
    heads_cast, merge_cast, expand_cast, shrink_cast = matrices
    head_dim = D // HEADS
    scale = head_dim ** (-0.5)
    split_shape = (SEQ, HEADS, head_dim)
    normed_one, unit_one, inverse_one = normalize(image, norm_gains[0], norm_shifts[0])
    normed_one = normed_one.astype(jnp.bfloat16)
    heads_matrix = heads_cast.reshape(D, 3 * D)
    projected = jnp.dot(normed_one, heads_matrix, preferred_element_type=jnp.float32).reshape(SEQ, 3, D)
    queries = (projected[:, 0] + attend_biases[0]).astype(jnp.bfloat16).reshape(split_shape)
    key_vecs = projected[:, 1].astype(jnp.bfloat16).reshape(split_shape)
    values = (projected[:, 2] + attend_biases[1]).astype(jnp.bfloat16).reshape(split_shape)
    scores = jnp.einsum('qhd,khd->hqk', queries.astype(jnp.float32), key_vecs.astype(jnp.float32)) * scale
    peak = lax.optimization_barrier(jnp.max(scores, axis=-1, keepdims=True))
    logsum = peak + jnp.log(lax.optimization_barrier(jnp.sum(jnp.exp(scores - peak), axis=-1, keepdims=True)))
    probs = jnp.exp(scores - logsum).astype(jnp.bfloat16)
    attended = jnp.einsum('hqk,khd->qhd', probs.astype(jnp.float32), values.astype(jnp.float32)).astype(jnp.bfloat16)
    attended_flat = attended.reshape(SEQ, D)
    middle = image + jnp.dot(attended_flat, merge_cast.T, preferred_element_type=jnp.float32) + branch_biases[0]
    normed_two, unit_two, inverse_two = normalize(middle, norm_gains[1], norm_shifts[1])
    normed_two = normed_two.astype(jnp.bfloat16)
    before = jnp.dot(normed_two, expand_cast, preferred_element_type=jnp.float32) + hidden_biases
    active = gelu_exact(before).astype(jnp.bfloat16)
    block_out = live * (middle + jnp.dot(active, shrink_cast.T, preferred_element_type=jnp.float32) + branch_biases[1])
    upstream = live * cotangent
    upstream_cast = upstream.astype(jnp.bfloat16)
    shrink_grad = jnp.dot(upstream_cast.T, active, preferred_element_type=jnp.float32)
    dactive = jnp.dot(upstream_cast, shrink_cast, preferred_element_type=jnp.float32)
    dbefore = jax.vjp(gelu_exact, before)[1](dactive)[0]
    dbefore_cast = dbefore.astype(jnp.bfloat16)
    expand_grad = jnp.dot(normed_two.T, dbefore_cast, preferred_element_type=jnp.float32)
    hidden_grad = lax.optimization_barrier(jnp.sum(dbefore, axis=0))
    dnormed_two = jnp.dot(dbefore_cast, expand_cast.T, preferred_element_type=jnp.float32)
    back_two, gain_two, shift_two = normalize_back(dnormed_two, unit_two, inverse_two, norm_gains[1])
    dmiddle = upstream + back_two
    dmiddle_cast = dmiddle.astype(jnp.bfloat16)
    merge_grad = jnp.dot(dmiddle_cast.T, attended_flat, preferred_element_type=jnp.float32)
    dattended = jnp.dot(dmiddle_cast, merge_cast, preferred_element_type=jnp.float32).astype(jnp.bfloat16).reshape(split_shape)
    dattended_wide = dattended.astype(jnp.float32)
    probs_again = jnp.exp(scores - logsum)
    dvalues = jnp.einsum('hqk,qhd->khd', probs.astype(jnp.float32), dattended_wide)
    dprobs = jnp.einsum('qhd,khd->hqk', dattended_wide, values.astype(jnp.float32))
    delta = jnp.einsum('qhd,qhd->hq', dattended_wide, attended.astype(jnp.float32))[:, :, None]
    dscores = (probs_again * (dprobs - delta) * scale).astype(jnp.bfloat16).astype(jnp.float32)
    dqueries = jnp.einsum('hqk,khd->qhd', dscores, key_vecs.astype(jnp.float32))
    dkeys = jnp.einsum('hqk,qhd->khd', dscores, queries.astype(jnp.float32))
    dproject = jnp.stack([dqueries.reshape(SEQ, D), dkeys.reshape(SEQ, D), dvalues.reshape(SEQ, D)], axis=1)
    attend_grad = jnp.stack([lax.optimization_barrier(jnp.sum(dproject[:, 0], axis=0)), lax.optimization_barrier(jnp.sum(dproject[:, 2], axis=0))])
    dproject_cast = dproject.astype(jnp.bfloat16).reshape(SEQ, 3 * D)
    heads_grad = jnp.dot(normed_one.T, dproject_cast, preferred_element_type=jnp.float32).reshape(D, 3, D)
    dnormed_one = jnp.dot(dproject_cast, heads_matrix.T, preferred_element_type=jnp.float32)
    back_one, gain_one, shift_one = normalize_back(dnormed_one, unit_one, inverse_one, norm_gains[0])
    input_grad = dmiddle + back_one
    gradients = (heads_grad, merge_grad, expand_grad, shrink_grad, jnp.stack([gain_one, gain_two]), jnp.stack([shift_one, shift_two]), jnp.stack([lax.optimization_barrier(jnp.sum(dmiddle, axis=0)), lax.optimization_barrier(jnp.sum(upstream, axis=0))]), attend_grad, hidden_grad)
    return (block_out, input_grad, gradients)

def reference(images, cotangent, counts, heads_weight, heads_first, heads_second, merge_weight, merge_first, merge_second, expand_weight, expand_first, expand_second, shrink_weight, shrink_first, shrink_second, norm_gains, gains_first, gains_second, norm_shifts, shifts_first, shifts_second, branch_biases, branch_first, branch_second, attend_biases, attend_first, attend_second, hidden_biases, hidden_first, hidden_second):
    matrices = (heads_weight.astype(jnp.bfloat16), merge_weight.astype(jnp.bfloat16), expand_weight.astype(jnp.bfloat16), shrink_weight.astype(jnp.bfloat16))
    slot_ids = jnp.arange(SLOTS, dtype=jnp.int32)
    owner_counts = counts[slot_ids // IMG_CAP]
    live_slots = (slot_ids % IMG_CAP < owner_counts).astype(jnp.float32)
    zero_grads = (jnp.zeros((D, 3, D), jnp.float32), jnp.zeros((D, D), jnp.float32), jnp.zeros((D, FF), jnp.float32), jnp.zeros((D, FF), jnp.float32), jnp.zeros((2, D), jnp.float32), jnp.zeros((2, D), jnp.float32), jnp.zeros((2, D), jnp.float32), jnp.zeros((2, D), jnp.float32), jnp.zeros((FF,), jnp.float32))

    def visit(totals, inputs):
        image, upstream, live = inputs

        def run(operand):
            return image_pass(image, upstream, live, matrices, norm_gains, norm_shifts, branch_biases, attend_biases, hidden_biases)

        def skip(operand):
            return (jnp.zeros((SEQ, D), jnp.float32), jnp.zeros((SEQ, D), jnp.float32), zero_grads)
        block_out, input_grad, gradients = lax.cond(live > 0.5, run, skip, 0)
        totals = jax.tree.map(jnp.add, totals, gradients)
        return (totals, (block_out, input_grad))
    totals, outputs = lax.scan(visit, zero_grads, (images, cotangent, live_slots))
    block_out, input_grad = outputs
    heads_grad, merge_grad, expand_grad, shrink_grad, gains_grad, shifts_grad, branch_grad, attend_grad, hidden_grad = totals
    heads_next, heads_mean, heads_square = adamw(heads_weight, heads_first, heads_second, heads_grad, matrix_rate, weight_decay)
    merge_next, merge_mean, merge_square = adamw(merge_weight, merge_first, merge_second, merge_grad, matrix_rate, weight_decay)
    expand_next, expand_mean, expand_square = adamw(expand_weight, expand_first, expand_second, expand_grad, matrix_rate, weight_decay)
    shrink_next, shrink_mean, shrink_square = adamw(shrink_weight, shrink_first, shrink_second, shrink_grad, matrix_rate, weight_decay)
    gains_next, gains_mean, gains_square = adamw(norm_gains, gains_first, gains_second, gains_grad, vector_rate, 0.0)
    shifts_next, shifts_mean, shifts_square = adamw(norm_shifts, shifts_first, shifts_second, shifts_grad, vector_rate, 0.0)
    branch_next, branch_mean, branch_square = adamw(branch_biases, branch_first, branch_second, branch_grad, vector_rate, 0.0)
    attend_next, attend_mean, attend_square = adamw(attend_biases, attend_first, attend_second, attend_grad, vector_rate, 0.0)
    hidden_next, hidden_mean, hidden_square = adamw(hidden_biases, hidden_first, hidden_second, hidden_grad, vector_rate, 0.0)
    return (block_out, input_grad, heads_grad, merge_grad, expand_grad, shrink_grad, gains_grad, shifts_grad, branch_grad, attend_grad, hidden_grad, heads_next, merge_next, expand_next, shrink_next, gains_next, shifts_next, branch_next, attend_next, hidden_next, heads_mean, merge_mean, expand_mean, shrink_mean, gains_mean, shifts_mean, branch_mean, attend_mean, hidden_mean, heads_square, merge_square, expand_square, shrink_square, gains_square, shifts_square, branch_square, attend_square, hidden_square)
```

```python
import functools

import jax
import jax.numpy as jnp
from jax import lax
from jax.experimental import pallas as pl
from jax.experimental.pallas import tpu as pltpu
from jax.sharding import PartitionSpec as P

HEADS = 12
LANES = 128
ROW_TILE = 16


beta_one = 0.9
beta_two = 0.999
adam_epsilon = 1e-08
adam_steps = 2
matrix_rate = 0.02
vector_rate = 0.15
weight_decay = 0.1
norm_epsilon = 1e-06


def normalize(rows, gain, shift):
    centred = rows - jnp.mean(rows, axis=-1, keepdims=True)
    inverse = lax.rsqrt(jnp.mean(centred * centred, axis=-1, keepdims=True) + norm_epsilon)
    unit = centred * inverse
    return (unit * gain + shift, unit, inverse)


def normalize_back(upstream, unit, inverse, gain):
    through = upstream * gain
    inner = (
        through
        - jnp.mean(through, axis=-1, keepdims=True)
        - unit * jnp.mean(through * unit, axis=-1, keepdims=True)
    )
    return inverse * inner


def gelu_exact(values):
    return jax.nn.gelu(values, approximate=False)


def adamw(weight, first, second, gradient, rate, decay_factor):
    first_new = beta_one * first + (1.0 - beta_one) * gradient
    second_new = beta_two * second + (1.0 - beta_two) * gradient * gradient
    first_hat = first_new / (1.0 - beta_one**adam_steps)
    second_hat = second_new / (1.0 - beta_two**adam_steps)
    weight_new = weight - rate * (
        first_hat / (jnp.sqrt(second_hat) + adam_epsilon) + decay_factor * weight
    )
    return (weight_new, first_new, second_new)


def contract_last(left, right):
    return lax.dot_general(
        left, right, (((1,), (1,)), ((), ())), preferred_element_type=jnp.float32
    )


def contract_first(left, right):
    return lax.dot_general(
        left, right, (((0,), (0,)), ((), ())), preferred_element_type=jnp.float32
    )


def head_masks(rows, head_dim):
    lane = lax.broadcasted_iota(jnp.int32, (rows, LANES), 1)
    return [
        (lane >= start) & (lane < start + head_dim) for start in range(0, LANES, head_dim)
    ]


def attend_kernel(
    seq_len,
    head_dim,
    image_ref,
    weights_ref,
    gains_ref,
    shifts_ref,
    biases_ref,
    normed_ref,
    project_ref,
    attended_ref,
    logsum_ref,
    merged_ref,
):
    rows = image_ref.shape[1]
    local_width = attended_ref.shape[1]
    scale = head_dim ** (-0.5)
    normed, _, _ = normalize(image_ref[0], gains_ref[0:1, :], shifts_ref[0:1, :])
    normed = normed.astype(jnp.bfloat16)
    normed_ref[...] = normed
    projected = jnp.dot(
        normed, weights_ref[:, : 3 * local_width], preferred_element_type=jnp.float32
    )
    project_ref[:, :local_width] = (projected[:, :local_width] + biases_ref[0:1, :]).astype(
        jnp.bfloat16
    )
    project_ref[:, local_width : 2 * local_width] = projected[
        :, local_width : 2 * local_width
    ].astype(jnp.bfloat16)
    project_ref[:, 2 * local_width :] = (projected[:, 2 * local_width :] + biases_ref[1:2, :]).astype(
        jnp.bfloat16
    )
    masks = head_masks(rows, head_dim)
    real = lax.broadcasted_iota(jnp.int32, (rows, rows), 1) < seq_len
    lane = lax.broadcasted_iota(jnp.int32, (rows, LANES), 1)
    logsums = jnp.zeros((rows, LANES), jnp.float32)
    head = 0
    for start in range(0, local_width, LANES):
        queries = project_ref[:, start : start + LANES]
        key_vecs = project_ref[:, local_width + start : local_width + start + LANES]
        values = project_ref[:, 2 * local_width + start : 2 * local_width + start + LANES]
        attended = jnp.zeros((rows, LANES), jnp.float32)
        for mask in masks:
            own = jnp.where(mask, queries, jnp.zeros_like(queries))
            scores = contract_last(own, key_vecs) * scale
            scores = jnp.where(real, scores, -1e30)
            peak = jnp.max(scores, axis=-1, keepdims=True)
            logsum = peak + jnp.log(jnp.sum(jnp.exp(scores - peak), axis=-1, keepdims=True))
            probs = jnp.exp(scores - logsum).astype(jnp.bfloat16)
            mixed = jnp.dot(probs, values, preferred_element_type=jnp.float32)
            attended = jnp.where(mask, mixed, attended)
            logsums = jnp.where(lane == head, logsum, logsums)
            head += 1
        attended_ref[:, start : start + LANES] = attended.astype(jnp.bfloat16)
    logsum_ref[...] = logsums
    merged_ref[...] = contract_last(attended_ref[...], weights_ref[:, 3 * local_width :]).astype(
        jnp.bfloat16
    )


def attend_forward(slot, seq_len, head_dim, padded, weights, gains, shifts, biases):
    _, rows, width = padded.shape
    local_width = biases.shape[1]

    def whole(array):
        return pl.BlockSpec(array.shape, lambda i: (0,) * array.ndim)

    outs = (
        jax.ShapeDtypeStruct((rows, width), jnp.bfloat16),
        jax.ShapeDtypeStruct((rows, 3 * local_width), jnp.bfloat16),
        jax.ShapeDtypeStruct((rows, local_width), jnp.bfloat16),
        jax.ShapeDtypeStruct((rows, LANES), jnp.float32),
        jax.ShapeDtypeStruct((rows, width), jnp.bfloat16),
    )
    return pl.pallas_call(
        functools.partial(attend_kernel, seq_len, head_dim),
        grid=(1,),
        in_specs=[
            pl.BlockSpec((1, rows, width), lambda i: (slot, 0, 0)),
            whole(weights),
            whole(gains),
            whole(shifts),
            whole(biases),
        ],
        out_specs=[whole(o) for o in outs],
        out_shape=outs,
        name="attend_forward",
        compiler_params=pltpu.CompilerParams(vmem_limit_bytes=40 << 20),
    )(padded, weights, gains, shifts, biases)


def attend_back_kernel(
    seq_len,
    head_dim,
    dmiddle_ref,
    weights_ref,
    image_ref,
    gains_ref,
    shifts_ref,
    normed_ref,
    project_ref,
    attended_ref,
    logsum_ref,
    dnormed_ref,
    grads_ref,
    biases_ref,
    norms_ref,
    total_ref,
    dproject_ref,
):
    step = pl.program_id(0)
    rows = image_ref.shape[1]
    local_width = attended_ref.shape[2]
    scale = head_dim ** (-0.5)
    dmiddle = dmiddle_ref[0]
    attended_all = attended_ref[0]
    dattended_all = jnp.dot(
        dmiddle, weights_ref[:, 3 * local_width :], preferred_element_type=jnp.float32
    ).astype(jnp.bfloat16)
    masks = head_masks(rows, head_dim)
    real = lax.broadcasted_iota(jnp.int32, (rows, rows), 1) < seq_len
    bias_rows = []
    head = 0
    for start in range(0, local_width, LANES):
        queries = project_ref[0, :, start : start + LANES]
        key_vecs = project_ref[0, :, local_width + start : local_width + start + LANES]
        values = project_ref[0, :, 2 * local_width + start : 2 * local_width + start + LANES]
        dattended = dattended_all[:, start : start + LANES]
        product = dattended.astype(jnp.float32) * attended_all[:, start : start + LANES].astype(
            jnp.float32
        )
        dqueries = jnp.zeros((rows, LANES), jnp.float32)
        dkeys = jnp.zeros((rows, LANES), jnp.float32)
        dvalues = jnp.zeros((rows, LANES), jnp.float32)
        for mask in masks:
            nothing = jnp.zeros_like(queries)
            scores = contract_last(jnp.where(mask, queries, nothing), key_vecs) * scale
            probs = jnp.exp(
                jnp.where(real, scores - logsum_ref[0, :, head : head + 1], -1e30)
            )
            dprobs = contract_last(jnp.where(mask, dattended, nothing), values)
            delta = jnp.sum(jnp.where(mask, product, 0.0), axis=-1, keepdims=True)
            dscores = (probs * (dprobs - delta) * scale).astype(jnp.bfloat16)
            dqueries = jnp.where(
                mask, jnp.dot(dscores, key_vecs, preferred_element_type=jnp.float32), dqueries
            )
            dkeys = jnp.where(mask, contract_first(dscores, queries), dkeys)
            dvalues = jnp.where(
                mask, contract_first(probs.astype(jnp.bfloat16), dattended), dvalues
            )
            head += 1
        dproject_ref[:, start : start + LANES] = dqueries.astype(jnp.bfloat16)
        dproject_ref[:, local_width + start : local_width + start + LANES] = dkeys.astype(
            jnp.bfloat16
        )
        dproject_ref[:, 2 * local_width + start : 2 * local_width + start + LANES] = dvalues.astype(
            jnp.bfloat16
        )
        bias_rows.append(
            (jnp.sum(dqueries, axis=0, keepdims=True), jnp.sum(dvalues, axis=0, keepdims=True))
        )
    dproject = dproject_ref[...]
    dnormed = contract_last(dproject, weights_ref[:, : 3 * local_width]).astype(jnp.bfloat16)
    dnormed_ref[0] = dnormed
    dnormed = dnormed.astype(jnp.float32)
    _, unit, _ = normalize(image_ref[0], gains_ref[0:1, :], shifts_ref[0:1, :])
    gain_row = jnp.sum(dnormed * unit, axis=0, keepdims=True)
    shift_row = jnp.sum(dnormed, axis=0, keepdims=True)
    heads_part = contract_first(normed_ref[0], dproject)
    merge_part = contract_first(dmiddle, attended_all)

    @pl.when(step == 0)
    def _():
        total_ref[:, : 3 * local_width] = heads_part
        total_ref[:, 3 * local_width :] = merge_part
        norms_ref[0:1, :] = gain_row
        norms_ref[1:2, :] = shift_row
        for index, (query_row, value_row) in enumerate(bias_rows):
            lanes = slice(index * LANES, (index + 1) * LANES)
            biases_ref[0:1, lanes] = query_row
            biases_ref[1:2, lanes] = value_row

    @pl.when(step > 0)
    def _():
        total_ref[:, : 3 * local_width] += heads_part
        total_ref[:, 3 * local_width :] += merge_part
        norms_ref[0:1, :] += gain_row
        norms_ref[1:2, :] += shift_row
        for index, (query_row, value_row) in enumerate(bias_rows):
            lanes = slice(index * LANES, (index + 1) * LANES)
            biases_ref[0:1, lanes] += query_row
            biases_ref[1:2, lanes] += value_row

    @pl.when(step == pl.num_programs(0) - 1)
    def _():
        grads_ref[...] = total_ref[...].astype(jnp.bfloat16)


def attend_backward(
    seq_len, head_dim, dmiddle, weights, padded, gains, shifts, normed, project, attended, logsum
):
    slots, rows, width = padded.shape
    local_width = attended.shape[2]

    def whole(array):
        return pl.BlockSpec(array.shape, lambda i: (0,) * array.ndim)

    def by_slot(array):
        return pl.BlockSpec((1,) + array.shape[1:], lambda i: (i, 0, 0))

    outs = (
        jax.ShapeDtypeStruct((slots, rows, width), jnp.bfloat16),
        jax.ShapeDtypeStruct(weights.shape, jnp.bfloat16),
        jax.ShapeDtypeStruct((2, local_width), jnp.float32),
        jax.ShapeDtypeStruct((2, width), jnp.float32),
    )
    return pl.pallas_call(
        functools.partial(attend_back_kernel, seq_len, head_dim),
        grid=(slots,),
        in_specs=[
            by_slot(dmiddle),
            whole(weights),
            by_slot(padded),
            whole(gains),
            whole(shifts),
            by_slot(normed),
            by_slot(project),
            by_slot(attended),
            by_slot(logsum),
        ],
        out_specs=[by_slot(outs[0]), whole(outs[1]), whole(outs[2]), whole(outs[3])],
        out_shape=outs,
        scratch_shapes=[
            pltpu.VMEM(weights.shape, jnp.float32),
            pltpu.VMEM((rows, 3 * local_width), jnp.bfloat16),
        ],
        name="attend_backward",
        compiler_params=pltpu.CompilerParams(vmem_limit_bytes=48 << 20),
    )(dmiddle, weights, padded, gains, shifts, normed, project, attended, logsum)


def swap(array, axis):
    size = lax.axis_size(axis)
    if size == 1:
        return jnp.zeros_like(array)
    return lax.ppermute(array, axis, [(i, i ^ 1) for i in range(size)])


def sum_all(array, axis):
    size = lax.axis_size(axis)
    if size & (size - 1):
        return lax.psum(array, axis)
    stride = 1
    while stride < size:
        array = array + lax.ppermute(array, axis, [(i, i ^ stride) for i in range(size)])
        stride *= 2
    return array


def body(
    images,
    cotangent,
    counts,
    heads_weight,
    heads_first,
    heads_second,
    merge_weight,
    merge_first,
    merge_second,
    expand_weight,
    expand_first,
    expand_second,
    shrink_weight,
    shrink_first,
    shrink_second,
    norm_gains,
    gains_first,
    gains_second,
    norm_shifts,
    shifts_first,
    shifts_second,
    branch_biases,
    branch_first,
    branch_second,
    attend_biases,
    attend_first,
    attend_second,
    hidden_biases,
    hidden_first,
    hidden_second,
):
    slot_count, seq_len, width = images.shape
    head_dim = width // HEADS
    local_width = heads_weight.shape[2]
    hidden_width = expand_weight.shape[1]
    padding = -seq_len % ROW_TILE
    padded_len = seq_len + padding
    rows = slot_count * padded_len
    position = lax.axis_index("dp")
    ranks = jnp.arange(counts.shape[0], dtype=jnp.int32)
    own_count = jnp.sum(jnp.where(ranks == position, counts, 0))
    live = (jnp.arange(slot_count, dtype=jnp.int32) < own_count).astype(jnp.float32)
    live = live[:, None, None]
    shard_rows = heads_weight.shape[0]
    first_part = jnp.concatenate(
        [heads_weight.reshape(shard_rows, 3 * local_width), merge_weight], axis=1
    ).astype(jnp.bfloat16)
    second_part = jnp.concatenate([expand_weight, shrink_weight], axis=1).astype(jnp.bfloat16)
    first_full = lax.all_gather(first_part, "dp", axis=0, tiled=True)
    second_full = lax.all_gather(second_part, "dp", axis=0, tiled=True)
    expand_full = second_full[:, :hidden_width]
    shrink_full = second_full[:, hidden_width:]
    spread = ((0, 0), (0, padding), (0, 0))
    padded = jnp.pad(images, spread)
    upstream = (live * jnp.pad(cotangent, spread)).reshape(rows, width)
    saved = []
    merged = []
    for slot in range(slot_count):
        outs = attend_forward(
            slot, seq_len, head_dim, padded, first_full, norm_gains, norm_shifts, attend_biases
        )
        other = swap(outs[4], "tensor")
        merged.append(outs[4].astype(jnp.float32) + other.astype(jnp.float32))
        saved.append(outs[:4])
    normed_one, project, attended, logsum = [jnp.stack(each) for each in zip(*saved)]
    middle = (padded + jnp.stack(merged) + branch_biases[0]).reshape(rows, width)
    normed_two, unit_two, inverse_two = normalize(middle, norm_gains[1], norm_shifts[1])
    normed_two = normed_two.astype(jnp.bfloat16)
    before = jnp.dot(normed_two, expand_full, preferred_element_type=jnp.float32) + hidden_biases
    active = gelu_exact(before).astype(jnp.bfloat16)
    feedforward = lax.reduce_precision(contract_last(active, shrink_full), 8, 7)
    feedforward = feedforward + swap(feedforward.astype(jnp.bfloat16), "tensor").astype(jnp.float32)
    block_out = (middle + feedforward + branch_biases[1]).reshape(padded.shape)
    block_out = live * block_out[:, :seq_len]
    upstream_cast = upstream.astype(jnp.bfloat16)
    shrink_grad = contract_first(upstream_cast, active)
    dactive = jnp.dot(upstream_cast, shrink_full, preferred_element_type=jnp.float32)
    dbefore = jax.vjp(gelu_exact, before)[1](dactive)[0]
    dbefore_cast = dbefore.astype(jnp.bfloat16)
    expand_grad = contract_first(normed_two, dbefore_cast)
    hidden_grad = jnp.sum(dbefore, axis=0)
    dnormed_two = lax.reduce_precision(contract_last(dbefore_cast, expand_full), 8, 7)
    dnormed_two = dnormed_two + swap(dnormed_two.astype(jnp.bfloat16), "tensor").astype(jnp.float32)
    second_grad = jnp.concatenate(
        [expand_grad.astype(jnp.bfloat16), shrink_grad.astype(jnp.bfloat16)], axis=1
    )
    second_shard = lax.psum_scatter(second_grad, "dp", scatter_dimension=0, tiled=True).astype(
        jnp.float32
    )
    dmiddle = upstream + normalize_back(dnormed_two, unit_two, inverse_two, norm_gains[1])
    gain_two = jnp.sum(dnormed_two * unit_two, axis=0)
    shift_two = jnp.sum(dnormed_two, axis=0)
    dmiddle_cast = dmiddle.astype(jnp.bfloat16).reshape(padded.shape)
    dnormed_one, first_grad, attend_grad, norm_sums = attend_backward(
        seq_len,
        head_dim,
        dmiddle_cast,
        first_full,
        padded,
        norm_gains,
        norm_shifts,
        normed_one,
        project,
        attended,
        logsum,
    )
    first_shard = lax.psum_scatter(first_grad, "dp", scatter_dimension=0, tiled=True).astype(
        jnp.float32
    )
    dnormed_one = dnormed_one.astype(jnp.float32) + swap(dnormed_one, "tensor").astype(jnp.float32)
    _, unit_one, inverse_one = normalize(images, norm_gains[0], norm_shifts[0])
    input_grad = dmiddle.reshape(padded.shape)[:, :seq_len] + normalize_back(
        dnormed_one[:, :seq_len], unit_one, inverse_one, norm_gains[0]
    )
    early = jnp.concatenate(
        [
            jnp.stack([gain_two, shift_two, jnp.sum(dmiddle, axis=0), jnp.sum(upstream, axis=0)]),
            hidden_grad.reshape(-1, width),
        ]
    )
    early = sum_all(early, "dp")
    hidden_total = early[4:].reshape(hidden_biases.shape)
    branch_total = early[2:4]
    norm_sums = norm_sums + swap(norm_sums, "tensor")
    late = jnp.concatenate([norm_sums, attend_grad.reshape(-1, width)])
    late = sum_all(late, "dp")
    gains_total = jnp.stack([late[0], early[0]])
    shifts_total = jnp.stack([late[1], early[1]])
    attend_total = late[2:].reshape(attend_biases.shape)
    heads_shard = first_shard[:, : 3 * local_width].reshape(heads_weight.shape)
    merge_shard = first_shard[:, 3 * local_width :]
    expand_shard = second_shard[:, :hidden_width]
    shrink_shard = second_shard[:, hidden_width:]
    heads_next, heads_mean, heads_square = adamw(
        heads_weight, heads_first, heads_second, heads_shard, matrix_rate, weight_decay
    )
    merge_next, merge_mean, merge_square = adamw(
        merge_weight, merge_first, merge_second, merge_shard, matrix_rate, weight_decay
    )
    expand_next, expand_mean, expand_square = adamw(
        expand_weight, expand_first, expand_second, expand_shard, matrix_rate, weight_decay
    )
    shrink_next, shrink_mean, shrink_square = adamw(
        shrink_weight, shrink_first, shrink_second, shrink_shard, matrix_rate, weight_decay
    )
    gains_next, gains_mean, gains_square = adamw(
        norm_gains, gains_first, gains_second, gains_total, vector_rate, 0.0
    )
    shifts_next, shifts_mean, shifts_square = adamw(
        norm_shifts, shifts_first, shifts_second, shifts_total, vector_rate, 0.0
    )
    branch_next, branch_mean, branch_square = adamw(
        branch_biases, branch_first, branch_second, branch_total, vector_rate, 0.0
    )
    attend_next, attend_mean, attend_square = adamw(
        attend_biases, attend_first, attend_second, attend_total, vector_rate, 0.0
    )
    hidden_next, hidden_mean, hidden_square = adamw(
        hidden_biases, hidden_first, hidden_second, hidden_total, vector_rate, 0.0
    )
    return (
        block_out,
        input_grad,
        heads_shard,
        merge_shard,
        expand_shard,
        shrink_shard,
        gains_total,
        shifts_total,
        branch_total,
        attend_total,
        hidden_total,
        heads_next,
        merge_next,
        expand_next,
        shrink_next,
        gains_next,
        shifts_next,
        branch_next,
        attend_next,
        hidden_next,
        heads_mean,
        merge_mean,
        expand_mean,
        shrink_mean,
        gains_mean,
        shifts_mean,
        branch_mean,
        attend_mean,
        hidden_mean,
        heads_square,
        merge_square,
        expand_square,
        shrink_square,
        gains_square,
        shifts_square,
        branch_square,
        attend_square,
        hidden_square,
    )


def solution(mesh):
    return jax.shard_map(
        body,
        mesh=mesh,
        in_specs=(
            P("dp", None, None),
            P("dp", None, None),
            P(),
            P("dp", None, "tensor"),
            P("dp", None, "tensor"),
            P("dp", None, "tensor"),
            P("dp", "tensor"),
            P("dp", "tensor"),
            P("dp", "tensor"),
            P("dp", "tensor"),
            P("dp", "tensor"),
            P("dp", "tensor"),
            P("dp", "tensor"),
            P("dp", "tensor"),
            P("dp", "tensor"),
            P(),
            P(),
            P(),
            P(),
            P(),
            P(),
            P(),
            P(),
            P(),
            P(None, "tensor"),
            P(None, "tensor"),
            P(None, "tensor"),
            P("tensor"),
            P("tensor"),
            P("tensor"),
        ),
        out_specs=(
            P("dp", None, None),
            P("dp", None, None),
            P("dp", None, "tensor"),
            P("dp", "tensor"),
            P("dp", "tensor"),
            P("dp", "tensor"),
            P(),
            P(),
            P(),
            P(None, "tensor"),
            P("tensor"),
            P("dp", None, "tensor"),
            P("dp", "tensor"),
            P("dp", "tensor"),
            P("dp", "tensor"),
            P(),
            P(),
            P(),
            P(None, "tensor"),
            P("tensor"),
            P("dp", None, "tensor"),
            P("dp", "tensor"),
            P("dp", "tensor"),
            P("dp", "tensor"),
            P(),
            P(),
            P(),
            P(None, "tensor"),
            P("tensor"),
            P("dp", None, "tensor"),
            P("dp", "tensor"),
            P("dp", "tensor"),
            P("dp", "tensor"),
            P(),
            P(),
            P(),
            P(None, "tensor"),
            P("tensor"),
        ),
        check_vma=False,
    )
```
